32 devices in a mesh: pb: 4 (over y, core), col: 8 (over z, x).
Axes of the slice: x: 2, y: 2, z: 4, core: 2. Of those that a mesh axis runs over, the one named last changes fastest.
Arguments:
- queries: bfloat16 [2048, 1024], P(('pb', 'col')), may hold values from -6 to 6
- weights: bfloat16 [128, 512, 1024], P(('pb', 'col')), may hold values from -0.1875 to 0.1875
- shortlist: int32 [2048, 16], P(('pb', 'col')), may hold values from 0 to 127, all different within a row; in each aligned block of 64 rows (0 to 63, 64 to 127, ...) at most 24 rows name the same one
- pos_rank: int32 [2048, 4], P(('pb', 'col')), may hold values from 0 to 15
- pos_label: int32 [2048, 4], P(('pb', 'col')), may hold values from 0 to 511
Outputs:
- grad_weights: bfloat16 [128, 512, 1024], P(('pb', 'col'))
- grad_queries: bfloat16 [2048, 1024], P(('pb', 'col'))
The draws below stay inside these ranges and needn't reach their ends.
Inputs may be any that keep to these rules, and one draw needn't show every extreme that they name: `shortlist`: each row names 16 different clusters. Among the 64 rows of one device no cluster is named more than 24 times, a bound that some block reaches.
All inputs are finite; a program needn't handle non-finite values.
Results may differ from the reference program's by a relative error of at most 0.012.
Values may be sent and summed in bfloat16 or wider, within the bound.
A program may use at most 128 MiB of HBM per device.

```python
import math
import jax
import jax.numpy as jnp
import numpy as np
from jax import lax

D = 1024
CSIZE = 512
K = 16
P_SIZE = 4
Q_DEV = 64
QUERIES = 2048
CLUSTERS = 128
CAP = 24
N_PB = 4
N_COL = 8


def plant(drawn, rng, smallest, largest):
    index_at = [jax.random.randint(jax.random.fold_in(rng, axis), (), 0, length) for axis, length in enumerate(drawn.shape)]
    longest = drawn.shape.index(max(drawn.shape))
    neighbour = index_at[:longest] + [(index_at[longest] + 1) % drawn.shape[longest]] + index_at[longest + 1:]
    return drawn.at[tuple(index_at)].set(smallest).at[tuple(neighbour)].set(largest)


def shard_levels(stream_key, shape, shards, least, top_value):
    def one(position, blocks):
        steps = jax.random.uniform(jax.random.fold_in(jax.random.fold_in(stream_key, 6), position), (blocks,), jnp.float32, least / len(shards), top_value / len(shards))
        return jnp.repeat(jnp.exp(steps), shape[position] // blocks).reshape((-1,) + (1,) * (len(shape) - position - 1))

    loudness = one(*shards[0])
    for cut in shards[1:]:
        loudness = loudness * one(*cut)
    return loudness


def shared_out(key, own, number, rows, number_of, top, limit, lean):
    order = jax.random.permutation(key, number_of)
    heavy_load, usual = load_shares(number_of, rows * top, limit, lean, True), load_shares(number_of, rows * top, limit, lean, False)
    places = jnp.arange(number_of)

    def named(sizes, offset_by):
        used = int((sizes > 0).sum())
        fixed = max(1, used // 4)
        moved = fixed + (places - fixed + offset_by * (used - fixed)) % max(1, number_of - fixed)
        return jnp.zeros((number_of,), jnp.int32).at[order[jnp.where(places < fixed, places, moved)]].set(jnp.asarray(sizes, jnp.int32))

    sizes = jnp.where(number % 4 == 0, named(heavy_load, number // 4), named(usual, number - number // 4 - 1))
    mixed = jax.random.permutation(jax.random.fold_in(own, 3), number_of)
    source_of, taker = mixed[0:number_of // 2 * 2:2], mixed[1:number_of // 2 * 2:2]
    room = jnp.minimum(sizes[source_of] - 1, limit - sizes[taker]) // 2
    room = jnp.where((source_of == order[0]) | (taker == order[0]) | (sizes[taker] == 0), 0, jnp.maximum(room, 0))
    moved = jax.random.randint(jax.random.fold_in(own, 4), (number_of // 2,), 0, 1 << 20) % (room + 1)
    sizes = sizes.at[source_of].add(-moved).at[taker].add(moved)
    items = jnp.searchsorted(jnp.cumsum(sizes), jnp.arange(rows * top), side="right").astype(jnp.int32)
    table = items.reshape(top, rows).T
    table = table[jax.random.permutation(jax.random.fold_in(own, 1), rows)]
    offset_by = jax.random.randint(jax.random.fold_in(own, 2), (rows, 1), 0, top)
    return jnp.take_along_axis(table, (jnp.arange(top)[None, :] + offset_by) % top, axis=1)


def load_shares(number_of, total, most, skew, full):
    weights = [(1 << 20) // math.isqrt(standing ** skew) + 1 for standing in range(1, number_of + 1)]
    largest = most if full else min(most, max(-(-total // number_of), total * weights[0] // sum(weights)))
    least = 1 if total - largest >= number_of - 1 else 0
    counts, rest = [largest] + [least] * (number_of - 1), total - largest - least * (number_of - 1)
    while rest > 0:
        movable = [i for i in range(1, number_of) if counts[i] < largest] or [i for i in range(1, number_of) if counts[i] < most]
        whole, left = sum([weights[i] for i in movable]), rest
        for i in movable:
            more = min(most - counts[i], max(1, left * weights[i] // whole), rest)
            counts[i] = counts[i] + more
            rest = rest - more
    return np.array(counts)


def scatter_about(own_key, dims, spread, bound, cuts=(), kind=jnp.bfloat16):
    result = spread * jax.random.normal(own_key, dims, jnp.float32)
    if cuts:
        result = result * shard_levels(own_key, dims, cuts, -0.22, 0.18)
    return jnp.clip(result, -bound, bound).astype(kind)


def setup_inputs(seed: int = 0) -> dict:
    key_list = jax.random.split(jax.random.key(seed), 6)
    queries = scatter_about(key_list[0], (QUERIES, D), 1.0, 6.0, ((0, 32),))
    weights = scatter_about(key_list[1], (CLUSTERS, CSIZE, D), D ** -0.5, 0.1875, ((0, 32),))
    shortlist_keys = jax.random.split(jax.random.fold_in(key_list[2], 1), QUERIES // Q_DEV)
    shortlist_turns = jax.random.permutation(jax.random.fold_in(key_list[2], 3), QUERIES // Q_DEV)
    shortlist = jax.vmap(lambda own, number: shared_out(jax.random.fold_in(key_list[2], 2), own, number, Q_DEV, CLUSTERS, K, CAP, 2))(shortlist_keys, shortlist_turns).reshape((QUERIES, K))
    pos_rank = plant(jax.random.randint(key_list[3], (QUERIES, P_SIZE), 0, K), jax.random.fold_in(key_list[3], 1), 0, K - 1).astype(jnp.int32)
    pos_label = plant(jax.random.randint(key_list[4], (QUERIES, P_SIZE), 0, CSIZE), jax.random.fold_in(key_list[4], 1), 0, CSIZE - 1).astype(jnp.int32)
    return dict(queries=queries, weights=weights, shortlist=shortlist, pos_rank=pos_rank, pos_label=pos_label)


def reference(queries, weights, shortlist, pos_rank, pos_label):
    total_pairs = QUERIES * K
    clusters_of = shortlist.reshape(-1).astype(jnp.int32)
    pair_ids = jnp.arange(total_pairs, dtype=jnp.int32)
    query_of = (pair_ids // K).astype(jnp.int32)
    rank_of = (pair_ids % K).astype(jnp.int32)
    order = jnp.argsort(clusters_of, stable=True).astype(jnp.int32)
    loads = jnp.bincount(clusters_of, length=CLUSTERS).astype(jnp.int32)
    offsets = (jnp.cumsum(loads) - loads).astype(jnp.int32)
    most_rows = N_PB * N_COL * CAP
    padded_order = jnp.concatenate([order, jnp.zeros((most_rows,), jnp.int32)])
    labels = jnp.arange(CSIZE, dtype=jnp.int32)

    def one_cluster(accum, cluster):
        picks = lax.dynamic_slice(padded_order, (offsets[cluster].astype(jnp.int32),), (most_rows,))
        live = jnp.arange(most_rows, dtype=jnp.int32) < loads[cluster]
        rows_query = query_of[picks]
        rows_rank = rank_of[picks]
        inputs = queries[rows_query].astype(jnp.float32)
        block = weights[cluster].astype(jnp.float32)
        scores = jnp.dot(inputs, block.T, preferred_element_type=jnp.float32)
        target = jnp.zeros(scores.shape, jnp.float32)
        for which in range(P_SIZE):
            same_rank = (pos_rank[rows_query, which] == rows_rank)[:, None]
            same_label = pos_label[rows_query, which][:, None] == labels[None, :]
            target = jnp.maximum(target, jnp.logical_and(same_rank, same_label).astype(jnp.float32))
        grads = jnp.where(live[:, None], jax.nn.sigmoid(scores) - target, 0.0).astype(jnp.bfloat16)
        grads_wide = lax.optimization_barrier(grads).astype(jnp.float32)
        grad_block = jnp.dot(grads_wide.T, inputs, preferred_element_type=jnp.float32).astype(jnp.bfloat16)
        part = jnp.dot(grads_wide, block, preferred_element_type=jnp.float32).astype(jnp.bfloat16)
        part = lax.optimization_barrier(part).astype(jnp.float32)
        accum = accum.at[rows_query].add(jnp.where(live[:, None], part, 0.0))
        return accum, grad_block

    start = jnp.zeros((QUERIES, D), jnp.float32)
    accum, grad_weights = lax.scan(one_cluster, start, jnp.arange(CLUSTERS, dtype=jnp.int32))
    return grad_weights, accum.astype(jnp.bfloat16)
```

```python
import functools

import jax
import jax.numpy as jnp
from jax import lax
from jax.experimental import pallas as pl
from jax.experimental.pallas import tpu as pltpu
from jax.sharding import PartitionSpec as P

META = 128
MESH = pl.DeviceIdType.MESH


def query_meta(shortlist, pos_rank, pos_label):
    top_count = shortlist.shape[1]
    rank_ids = lax.broadcasted_iota(jnp.int32, (1, 1, top_count), 2)
    chosen = jnp.sum(jnp.where(pos_rank[:, :, None] == rank_ids, shortlist[:, None, :], 0), axis=2)
    fields = [shortlist // 256, shortlist % 256, chosen // 256, chosen % 256]
    fields += [pos_label // 256, pos_label % 256]
    packed = jnp.concatenate(fields, axis=1)
    packed = jnp.pad(packed, ((0, 0), (0, META - packed.shape[1])))
    return packed.astype(jnp.float32).astype(jnp.bfloat16)


def gradient_block(meta, scores, first_cluster, owned, labels, top_count, positives):
    meta = meta.astype(jnp.float32)
    first = first_cluster.astype(jnp.float32)
    t, p = top_count, positives
    named = meta[:, :t] * 256.0 + meta[:, t : 2 * t] - first
    base = 2 * t
    at_cluster = meta[:, base : base + p] * 256.0 + meta[:, base + p : base + 2 * p] - first
    at_label = meta[:, base + 2 * p : base + 3 * p] * 256.0 + meta[:, base + 3 * p : base + 4 * p]
    places = (at_cluster * labels + at_label).astype(jnp.int32)
    label_ids = lax.broadcasted_iota(jnp.int32, (1, labels), 1)
    columns = []
    for j in range(owned):
        live = jnp.max((named == float(j)).astype(jnp.float32), axis=1, keepdims=True)
        hit = None
        for w in range(p):
            same = (places[:, w : w + 1] - j * labels) == label_ids
            hit = same if hit is None else jnp.logical_or(hit, same)
        part = scores[:, j * labels : (j + 1) * labels]
        sig = 0.5 * jnp.tanh(0.5 * part) + 0.5
        columns.append(((sig - hit.astype(jnp.float32)) * live).astype(jnp.bfloat16))
    return jnp.concatenate(columns, axis=1)


def dense_kernel(owned, labels, top_count, positives, q_ref, m_ref, w_ref, gw_ref, part_ref, acc):
    step = pl.program_id(0)
    me = lax.axis_index("pb") * lax.axis_size("col") + lax.axis_index("col")

    @pl.when(step == 0)
    def _():
        acc[...] = jnp.zeros_like(acc)

    q = q_ref[...]
    scores = lax.dot_general(q, w_ref[...], (((1,), (1,)), ((), ())), preferred_element_type=jnp.float32)
    g = gradient_block(m_ref[...], scores, me * owned, owned, labels, top_count, positives)
    part_ref[...] = jnp.dot(g, w_ref[...], preferred_element_type=jnp.float32).astype(jnp.bfloat16)
    acc[...] += lax.dot_general(g, q, (((0,), (0,)), ((), ())), preferred_element_type=jnp.float32)

    @pl.when(step == pl.num_programs(0) - 1)
    def _():
        gw_ref[...] = acc[...].astype(jnp.bfloat16)


def plain_body(queries, weights, shortlist, pos_rank, pos_label):
    rows, width = queries.shape
    owned, labels, _ = weights.shape
    pb_count, col_count = lax.axis_size("pb"), lax.axis_size("col")
    devices = pb_count * col_count
    sent = jnp.concatenate([queries, query_meta(shortlist, pos_rank, pos_label)], axis=1)
    everyone = lax.all_gather(sent, ("pb", "col"), axis=0, tiled=True)
    total = devices * rows
    block = 256
    grad_weights, part = pl.pallas_call(
        functools.partial(dense_kernel, owned, labels, shortlist.shape[1], pos_rank.shape[1]),
        grid=(total // block,),
        in_specs=[
            pl.BlockSpec((block, width), lambda i: (i, 0)),
            pl.BlockSpec((block, META), lambda i: (i, width // META)),
            pl.BlockSpec((owned * labels, width), lambda i: (0, 0)),
        ],
        out_specs=[
            pl.BlockSpec((owned * labels, width), lambda i: (0, 0)),
            pl.BlockSpec((block, width), lambda i: (i, 0)),
        ],
        out_shape=[
            jax.ShapeDtypeStruct((owned * labels, width), jnp.bfloat16),
            jax.ShapeDtypeStruct((total, width), jnp.bfloat16),
        ],
        scratch_shapes=[pltpu.VMEM((owned * labels, width), jnp.float32)],
        compiler_params=pltpu.CompilerParams(vmem_limit_bytes=60 * 1024 * 1024),
    )(everyone, everyone, weights.reshape(owned * labels, width))
    part = part.reshape(pb_count, col_count, rows, width)
    part = lax.all_to_all(part, "pb", split_axis=0, concat_axis=0, tiled=True)
    part = jnp.sum(part, axis=0, dtype=jnp.float32).astype(jnp.bfloat16)
    part = lax.all_to_all(part, "col", split_axis=0, concat_axis=0, tiled=True)
    grad_queries = jnp.sum(part, axis=0, dtype=jnp.float32).astype(jnp.bfloat16)
    return grad_weights.reshape(weights.shape), grad_queries


def dot(a, b, ca, cb):
    return lax.dot_general(a, b, (((ca,), (cb,)), ((), ())), preferred_element_type=jnp.float32)


def add_rounded(a, b):
    return (a.astype(jnp.float32) + b.astype(jnp.float32)).astype(jnp.bfloat16)


STEPS = 4
ROWS = 64
CHUNK = 256
WIDTH = 1024
LABELS = 512
OWNED = 4
TOTAL = 2048
TILES = 32


def fused_kernel(
    q_ref, sl_ref, pr_ref, lab_ref, w_hbm,
    gw_hbm, gq_ref,
    own_q, sib_q, all_q, w_all, g_all, gw_all,
    sib_out, sib_in, plane, s_in, pair, f_in, single, z_in,
    ag_send, own_recv, sib_recv, rs_send, rs_recv, w_sem, gw_sem,
):
    pb, col = lax.axis_index("pb"), lax.axis_index("col")
    core, y = pb % 2, pb // 2
    x, z = col % 2, col // 2
    flip_y, flip_x = (pb + 2) % 4, col + 1 - 2 * x
    first = (pb + core * (flip_y - pb), col + (1 - core) * (flip_x - col))
    second = (pb + (1 - core) * (flip_y - pb), col + core * (flip_x - col))
    sibling = (pb + 1 - 2 * core, col)
    zs = [z, z + 1 - 2 * (z % 2), (z + 2) % 4, 3 - z]
    across = [None] + [(pb, zs[k] * 2 + x) for k in (1, 2, 3)]
    me = pb * lax.axis_size("col") + col

    w_copy = pltpu.make_async_copy(w_hbm, w_all, w_sem)
    w_copy.start()

    barrier = pltpu.get_barrier_semaphore()
    partners = [first, second, sibling] + across[1:]
    for partner in partners:
        pl.semaphore_signal(barrier, inc=1, device_id=partner, device_id_type=MESH)

    half = (q_ref[...].astype(jnp.float32) * 0.5).astype(jnp.bfloat16)
    for d in range(WIDTH // 128):
        own_q[0, 0, 0, 4 * d : 4 * d + 4] = half[:, 128 * d : 128 * (d + 1)].reshape(4, 16, 128)
    named = sl_ref[...]
    lanes = lax.broadcasted_iota(jnp.int32, (ROWS, 128), 1)
    fields = jnp.zeros((ROWS, 128), jnp.int32)
    rank_ids = lax.broadcasted_iota(jnp.int32, (1, 16), 1)
    for t in range(16):
        fields = jnp.where(lanes == t, named[:, t : t + 1], fields)
    for j in range(4):
        chosen = jnp.sum(jnp.where(pr_ref[:, j : j + 1] == rank_ids, named, 0), axis=1, keepdims=True)
        place = chosen * LABELS + lab_ref[:, j : j + 1]
        fields = jnp.where(lanes == 16 + j, place >> 8, fields)
        fields = jnp.where(lanes == 20 + j, place & 255, fields)
    fields = fields.astype(jnp.float32)
    tile = fields[0:16]
    for g in range(1, 4):
        tile = tile + pltpu.roll(fields[16 * g : 16 * g + 16], 32 * g, 1)
    own_q[0, 0, 0, TILES] = tile.astype(jnp.bfloat16)

    pl.semaphore_wait(barrier, len(partners))

    sends = []

    def send(src, dst, send_sem, recv_sem, device):
        copy = pltpu.make_async_remote_copy(
            src_ref=src, dst_ref=dst, send_sem=send_sem, recv_sem=recv_sem, device_id=device, device_id_type=MESH
        )
        copy.start()
        sends.append(copy)

    def landed(ref, recv_sem):
        pltpu.make_async_remote_copy(
            src_ref=ref, dst_ref=ref, send_sem=w_sem, recv_sem=recv_sem, device_id=sibling, device_id_type=MESH
        ).wait_recv()

    def spread(k, s, f, how):
        src = own_q.at[k, s, f]
        for way in how:
            n = len(sends)
            if way == "f":
                send(src, own_q.at[k, s, 1], ag_send.at[n], own_recv.at[k, s, 1], first)
            elif way == "s":
                send(src, own_q.at[k, 1, f], ag_send.at[n], own_recv.at[k, 1, f], second)
            elif way == "b":
                send(src, sib_q.at[k, s, f], ag_send.at[n], sib_recv.at[k, s, f], sibling)
            else:
                to = int(way)
                send(src, own_q.at[to, 0, 0], ag_send.at[n], own_recv.at[to, 0, 0], across[to])

    def got(k, s, f, how):
        landed(own_q.at[k, s, f], own_recv.at[k, s, f])
        spread(k, s, f, how)

    def got_sib(k):
        for s in range(2):
            for f in range(2):
                landed(sib_q.at[k, s, f], sib_recv.at[k, s, f])

    def chunk(k, side):
        return (2 * k + side) * CHUNK

    def scores(blocks, k, side):
        base = chunk(k, side)
        parts = []
        for b in range(4):
            block = blocks[k, b // 2, b % 2]
            lanes_of = [block[4 * d : 4 * d + 4].reshape(ROWS, 128) for d in range(WIDTH // 128)]
            all_q[base + ROWS * b : base + ROWS * (b + 1), :] = jnp.concatenate(lanes_of, axis=1)
            meta = block[TILES].astype(jnp.float32)
            parts += [meta] + [pltpu.roll(meta, 128 - 32 * g, 1) for g in range(1, 4)]
        meta = jnp.concatenate(parts, axis=0)
        lane = lax.broadcasted_iota(jnp.int32, (1, 128), 1)
        names = jnp.where(lane < 16, meta, -1.0)
        places = (meta * 256.0 + pltpu.roll(meta, 128 - 4, 1)).astype(jnp.int32) - me * (OWNED * LABELS)
        q = all_q[base : base + CHUNK, :]
        ids = lax.broadcasted_iota(jnp.int32, (1, LABELS), 1)
        for j in range(OWNED):
            same = (names == (me * OWNED + j).astype(jnp.float32)).astype(jnp.float32)
            live = 0.5 * jnp.max(same, axis=1, keepdims=True)
            hit = None
            for w in range(4):
                one = places[:, 16 + w : 17 + w] == ids + j * LABELS
                hit = one if hit is None else jnp.logical_or(hit, one)
            s = dot(q, w_all[j * LABELS : (j + 1) * LABELS, :], 1, 1)
            g = live * jnp.tanh(s) + jnp.where(hit, live - 1.0, live)
            g_all[base : base + CHUNK, j * LABELS : (j + 1) * LABELS] = g.astype(jnp.bfloat16)

    def partial(k, side):
        base = chunk(k, side)
        return dot(g_all[base : base + CHUNK, :], w_all[...], 1, 0)

    def rs(kind, k, src, dst, device):
        send(src, dst, rs_send.at[kind, k], rs_recv.at[kind, k], device)

    def part_sib(k):
        sib_out[k] = partial(k, 0).astype(jnp.bfloat16)
        rs(0, k, sib_out.at[k], sib_in.at[k], sibling)

    def part_own(k):
        landed(sib_in.at[k], rs_recv.at[0, k])
        plane[k] = (partial(k, 1) + sib_in[k].astype(jnp.float32)).astype(jnp.bfloat16)
        rs(1, k, plane.at[k, pl.ds(2 * ROWS, 2 * ROWS)], s_in.at[k], second)

    def sum_second(k):
        landed(s_in.at[k], rs_recv.at[1, k])
        pair[k] = add_rounded(plane[k, : 2 * ROWS], s_in[k])
        rs(2, k, pair.at[k, pl.ds(ROWS, ROWS)], f_in.at[k], first)

    def sum_first(k):
        landed(f_in.at[k], rs_recv.at[2, k])
        single[k] = add_rounded(pair[k, :ROWS], f_in[k])
        if k:
            rs(3, k, single.at[k], z_in.at[k], across[k])

    gw_copies = []

    def weights_tile(j):
        rows = CHUNK
        r = dot(g_all[:, j * rows : (j + 1) * rows], all_q[...], 0, 0)
        gw_all[j * rows : (j + 1) * rows, :] = (r * 2.0).astype(jnp.bfloat16)
        copy = pltpu.make_async_copy(
            gw_all.at[pl.ds(j * rows, rows)], gw_hbm.at[pl.ds(j * rows, rows)], gw_sem.at[j]
        )
        copy.start()
        gw_copies.append(copy)

    spread(0, 0, 0, "fs1b23")
    got(0, 0, 1, "sb")
    got(1, 0, 0, "fsb")
    got(0, 1, 0, "b")
    w_copy.wait()
    got(0, 1, 1, "b")
    got(1, 0, 1, "sb")
    got_sib(0)
    scores(sib_q, 0, 0)
    got(2, 0, 0, "fsb")
    part_sib(0)
    got(1, 1, 0, "b")
    scores(own_q, 0, 1)
    got(1, 1, 1, "b")
    got(2, 0, 1, "sb")
    part_own(0)
    got(3, 0, 0, "fsb")
    got_sib(1)
    scores(sib_q, 1, 0)
    got(2, 1, 0, "b")
    part_sib(1)
    got(2, 1, 1, "b")
    got(3, 0, 1, "sb")
    scores(own_q, 1, 1)
    sum_second(0)
    part_own(1)
    got_sib(2)
    scores(sib_q, 2, 0)
    got(3, 1, 0, "b")
    part_sib(2)
    sum_first(0)
    scores(own_q, 2, 1)
    got(3, 1, 1, "b")
    sum_second(1)
    part_own(2)
    got_sib(3)
    scores(sib_q, 3, 0)
    sum_first(1)
    part_sib(3)
    sum_second(2)
    scores(own_q, 3, 1)
    sum_first(2)
    part_own(3)
    weights_tile(0)
    weights_tile(1)
    weights_tile(2)
    sum_second(3)
    weights_tile(3)
    weights_tile(4)
    sum_first(3)
    weights_tile(5)
    weights_tile(6)
    weights_tile(7)
    total = single[0].astype(jnp.float32)
    for k in (1, 2, 3):
        landed(z_in.at[k], rs_recv.at[3, k])
        total = total + z_in[k].astype(jnp.float32)
    gq_ref[...] = total.astype(jnp.bfloat16)
    for copy in sends:
        copy.wait_send()
    for copy in gw_copies:
        copy.wait()


def fused_body(queries, weights, shortlist, pos_rank, pos_label):
    vmem = pl.BlockSpec(memory_space=pltpu.VMEM)
    anywhere = pl.BlockSpec(memory_space=pl.ANY)
    bf16 = jnp.bfloat16
    grad_weights, grad_queries = pl.pallas_call(
        fused_kernel,
        in_specs=[vmem] * 4 + [anywhere],
        out_specs=[anywhere, vmem],
        out_shape=[
            jax.ShapeDtypeStruct((OWNED * LABELS, WIDTH), bf16),
            jax.ShapeDtypeStruct((ROWS, WIDTH), bf16),
        ],
        scratch_shapes=[
            pltpu.VMEM((STEPS, 2, 2, TILES + 1, 16, 128), bf16),
            pltpu.VMEM((STEPS, 2, 2, TILES + 1, 16, 128), bf16),
            pltpu.VMEM((TOTAL, WIDTH), bf16),
            pltpu.VMEM((OWNED * LABELS, WIDTH), bf16),
            pltpu.VMEM((TOTAL, OWNED * LABELS), bf16),
            pltpu.VMEM((OWNED * LABELS, WIDTH), bf16),
            pltpu.VMEM((STEPS, CHUNK, WIDTH), bf16),
            pltpu.VMEM((STEPS, CHUNK, WIDTH), bf16),
            pltpu.VMEM((STEPS, CHUNK, WIDTH), bf16),
            pltpu.VMEM((STEPS, 2 * ROWS, WIDTH), bf16),
            pltpu.VMEM((STEPS, 2 * ROWS, WIDTH), bf16),
            pltpu.VMEM((STEPS, ROWS, WIDTH), bf16),
            pltpu.VMEM((STEPS, ROWS, WIDTH), bf16),
            pltpu.VMEM((STEPS, ROWS, WIDTH), bf16),
            pltpu.SemaphoreType.DMA((48,)),
            pltpu.SemaphoreType.DMA((STEPS, 2, 2)),
            pltpu.SemaphoreType.DMA((STEPS, 2, 2)),
            pltpu.SemaphoreType.DMA((4, STEPS)),
            pltpu.SemaphoreType.DMA((4, STEPS)),
            pltpu.SemaphoreType.DMA,
            pltpu.SemaphoreType.DMA((8,)),
        ],
        cost_estimate=pl.CostEstimate(
            flops=6 * TOTAL * OWNED * LABELS * WIDTH, bytes_accessed=12 << 20, transcendentals=TOTAL * OWNED * LABELS
        ),
        compiler_params=pltpu.CompilerParams(
            collective_id=0, has_side_effects=True, vmem_limit_bytes=56 * 1024 * 1024
        ),
    )(queries, shortlist, pos_rank, pos_label, weights.reshape(OWNED * LABELS, WIDTH))
    return grad_weights.reshape(weights.shape), grad_queries


def body(queries, weights, shortlist, pos_rank, pos_label):
    sizes = (lax.axis_size("pb"), lax.axis_size("col")) + queries.shape + weights.shape
    sizes += (shortlist.shape[1], pos_rank.shape[1])
    if sizes == (4, 8, ROWS, WIDTH, OWNED, LABELS, WIDTH, 16, 4):
        return fused_body(queries, weights, shortlist, pos_rank, pos_label)
    return plain_body(queries, weights, shortlist, pos_rank, pos_label)


def solution(mesh):
    return jax.shard_map(
        body,
        mesh=mesh,
        in_specs=(
            P(("pb", "col"), None),
            P(("pb", "col"), None, None),
            P(("pb", "col"), None),
            P(("pb", "col"), None),
            P(("pb", "col"), None),
        ),
        out_specs=(P(("pb", "col"), None, None), P(("pb", "col"), None)),
        check_vma=False,
    )
```

```python
import functools

import jax
import jax.numpy as jnp
from jax import lax
from jax.experimental import pallas as pl
from jax.experimental.pallas import tpu as pltpu
from jax.sharding import PartitionSpec as P

META = 128
MESH = pl.DeviceIdType.MESH


def query_meta(shortlist, pos_rank, pos_label):
    top_count = shortlist.shape[1]
    rank_ids = lax.broadcasted_iota(jnp.int32, (1, 1, top_count), 2)
    chosen = jnp.sum(jnp.where(pos_rank[:, :, None] == rank_ids, shortlist[:, None, :], 0), axis=2)
    fields = [shortlist // 256, shortlist % 256, chosen // 256, chosen % 256]
    fields += [pos_label // 256, pos_label % 256]
    packed = jnp.concatenate(fields, axis=1)
    packed = jnp.pad(packed, ((0, 0), (0, META - packed.shape[1])))
    return packed.astype(jnp.float32).astype(jnp.bfloat16)


def gradient_block(meta, scores, first_cluster, owned, labels, top_count, positives):
    meta = meta.astype(jnp.float32)
    first = first_cluster.astype(jnp.float32)
    t, p = top_count, positives
    named = meta[:, :t] * 256.0 + meta[:, t : 2 * t] - first
    base = 2 * t
    at_cluster = meta[:, base : base + p] * 256.0 + meta[:, base + p : base + 2 * p] - first
    at_label = meta[:, base + 2 * p : base + 3 * p] * 256.0 + meta[:, base + 3 * p : base + 4 * p]
    places = (at_cluster * labels + at_label).astype(jnp.int32)
    label_ids = lax.broadcasted_iota(jnp.int32, (1, labels), 1)
    columns = []
    for j in range(owned):
        live = jnp.max((named == float(j)).astype(jnp.float32), axis=1, keepdims=True)
        hit = None
        for w in range(p):
            same = (places[:, w : w + 1] - j * labels) == label_ids
            hit = same if hit is None else jnp.logical_or(hit, same)
        part = scores[:, j * labels : (j + 1) * labels]
        sig = 0.5 * jnp.tanh(0.5 * part) + 0.5
        columns.append(((sig - hit.astype(jnp.float32)) * live).astype(jnp.bfloat16))
    return jnp.concatenate(columns, axis=1)


def dense_kernel(owned, labels, top_count, positives, q_ref, m_ref, w_ref, gw_ref, part_ref, acc):
    step = pl.program_id(0)
    me = lax.axis_index("pb") * lax.axis_size("col") + lax.axis_index("col")

    @pl.when(step == 0)
    def _():
        acc[...] = jnp.zeros_like(acc)

    q = q_ref[...]
    scores = lax.dot_general(q, w_ref[...], (((1,), (1,)), ((), ())), preferred_element_type=jnp.float32)
    g = gradient_block(m_ref[...], scores, me * owned, owned, labels, top_count, positives)
    part_ref[...] = jnp.dot(g, w_ref[...], preferred_element_type=jnp.float32).astype(jnp.bfloat16)
    acc[...] += lax.dot_general(g, q, (((0,), (0,)), ((), ())), preferred_element_type=jnp.float32)

    @pl.when(step == pl.num_programs(0) - 1)
    def _():
        gw_ref[...] = acc[...].astype(jnp.bfloat16)


def plain_body(queries, weights, shortlist, pos_rank, pos_label):
    rows, width = queries.shape
    owned, labels, _ = weights.shape
    pb_count, col_count = lax.axis_size("pb"), lax.axis_size("col")
    devices = pb_count * col_count
    sent = jnp.concatenate([queries, query_meta(shortlist, pos_rank, pos_label)], axis=1)
    everyone = lax.all_gather(sent, ("pb", "col"), axis=0, tiled=True)
    total = devices * rows
    block = 256
    grad_weights, part = pl.pallas_call(
        functools.partial(dense_kernel, owned, labels, shortlist.shape[1], pos_rank.shape[1]),
        grid=(total // block,),
        in_specs=[
            pl.BlockSpec((block, width), lambda i: (i, 0)),
            pl.BlockSpec((block, META), lambda i: (i, width // META)),
            pl.BlockSpec((owned * labels, width), lambda i: (0, 0)),
        ],
        out_specs=[
            pl.BlockSpec((owned * labels, width), lambda i: (0, 0)),
            pl.BlockSpec((block, width), lambda i: (i, 0)),
        ],
        out_shape=[
            jax.ShapeDtypeStruct((owned * labels, width), jnp.bfloat16),
            jax.ShapeDtypeStruct((total, width), jnp.bfloat16),
        ],
        scratch_shapes=[pltpu.VMEM((owned * labels, width), jnp.float32)],
        compiler_params=pltpu.CompilerParams(vmem_limit_bytes=60 * 1024 * 1024),
    )(everyone, everyone, weights.reshape(owned * labels, width))
    part = part.reshape(pb_count, col_count, rows, width)
    part = lax.all_to_all(part, "pb", split_axis=0, concat_axis=0, tiled=True)
    part = jnp.sum(part, axis=0, dtype=jnp.float32).astype(jnp.bfloat16)
    part = lax.all_to_all(part, "col", split_axis=0, concat_axis=0, tiled=True)
    grad_queries = jnp.sum(part, axis=0, dtype=jnp.float32).astype(jnp.bfloat16)
    return grad_weights.reshape(weights.shape), grad_queries


def dot(a, b, ca, cb):
    return lax.dot_general(a, b, (((ca,), (cb,)), ((), ())), preferred_element_type=jnp.float32)


def add_rounded(a, b):
    return (a.astype(jnp.float32) + b.astype(jnp.float32)).astype(jnp.bfloat16)


STEPS = 4
ROWS = 64
CHUNK = 256
WIDTH = 1024
LABELS = 512
OWNED = 4
TOTAL = 2048
TILES = 32


SCHEDULE = (
    "0001", "000s", "000b", "000f", "0002", "010b", "001s", "100f", "001b", "100s", "100b", "0003", "011b", "200b",
    "so0", "200f", "ss0", "101s", "ps0", "101b", "110b", "201s", "201b", "200s", "111b", "so1", "300f", "ss1", "210b",
    "211b", "300s", "ps1", "301s", "ss2", "310b", "po1", "ps2", "301b", "so2", "pp1", "300b", "311b", "po2", "ss3",
    "pp2", "s21", "ps3", "s22", "so3", "po3", "po0", "s12", "pp3", "w6", "s23", "s11", "w7", "w2", "s20", "pp0",
    "s13", "w5", "w1", "w4", "w3", "w0", "s10",
)


def fused_kernel(
    q_ref, sl_ref, pr_ref, lab_ref, w_hbm,
    gw_out, gq_out,
    own_q, sib_q, all_q, w_all, g_all,
    sib_out, sib_in, plane, s_in, pair, f_in, single, z_in,
    ag_send, own_recv, sib_recv, rs_send, rs_recv, w_sem,
):
    pb, col = lax.axis_index("pb"), lax.axis_index("col")
    core = pb % 2
    x, z = col % 2, col // 2
    flip_y, flip_x = (pb + 2) % 4, col + 1 - 2 * x
    first = (pb + core * (flip_y - pb), col + (1 - core) * (flip_x - col))
    second = (pb + (1 - core) * (flip_y - pb), col + core * (flip_x - col))
    sibling = (pb + 1 - 2 * core, col)
    zs = [z, z + 1 - 2 * (z % 2), (z + 2) % 4, 3 - z]
    across = [None] + [(pb, zs[k] * 2 + x) for k in (1, 2, 3)]
    me = pb * lax.axis_size("col") + col

    barrier = pltpu.get_barrier_semaphore()
    partners = [first, second, sibling] + across[1:]
    for partner in partners:
        pl.semaphore_signal(barrier, inc=1, device_id=partner, device_id_type=MESH)

    w_copy = pltpu.make_async_copy(w_hbm, w_all, w_sem)
    w_copy.start()

    half = (q_ref[...].astype(jnp.float32) * 0.5).astype(jnp.bfloat16)
    for d in range(WIDTH // 128):
        own_q[0, 0, 0, 4 * d : 4 * d + 4] = half[:, 128 * d : 128 * (d + 1)].reshape(4, 16, 128)
    named = sl_ref[...]
    rank_ids = lax.broadcasted_iota(jnp.int32, (16, 1), 0)
    rows_of = lax.broadcasted_iota(jnp.int32, (8, 1), 0)
    places = jnp.zeros((8, ROWS), jnp.int32)
    for j in range(4):
        chosen = jnp.sum(jnp.where(pr_ref[j : j + 1, :] == rank_ids, named, 0), axis=0, keepdims=True)
        place = chosen * LABELS + lab_ref[j : j + 1, :]
        places = jnp.where(rows_of == j, place >> 8, places)
        places = jnp.where(rows_of == 4 + j, place & 255, places)
    fields = jnp.concatenate([named, places, jnp.zeros((104, ROWS), jnp.int32)], axis=0).astype(jnp.float32)
    fields = jnp.concatenate([fields, jnp.zeros((128, 128 - ROWS), jnp.float32)], axis=1).T
    tile = fields[0:16]
    for g in range(1, 4):
        tile = tile + pltpu.roll(fields[16 * g : 16 * g + 16], 32 * g, 1)
    own_q[0, 0, 0, TILES] = tile.astype(jnp.bfloat16)

    pl.semaphore_wait(barrier, len(partners))

    def remote(src, dst, send_sem, recv_sem, device):
        return pltpu.make_async_remote_copy(
            src_ref=src, dst_ref=dst, send_sem=send_sem, recv_sem=recv_sem, device_id=device, device_id_type=MESH
        )

    def landed(ref, recv_sem):
        remote(ref, ref, w_sem, recv_sem, sibling).wait_recv()

    def all_sent(ref, send_sem):
        remote(ref, ref, send_sem, w_sem, sibling).wait_send()

    arrived = []

    def arrive(k, s, f):
        if k + s + f and not any(done == (k, s, f) for done in arrived):
            arrived.append((k, s, f))
            landed(own_q.at[k, s, f], own_recv.at[k, s, f])

    def forward(k, s, f, way):
        arrive(k, s, f)
        src = own_q.at[k, s, f]
        if way == "f":
            remote(src, own_q.at[k, s, 1], ag_send.at[0], own_recv.at[k, s, 1], first).start()
        elif way == "s":
            remote(src, own_q.at[k, 1, f], ag_send.at[1], own_recv.at[k, 1, f], second).start()
        elif way == "b":
            remote(src, sib_q.at[k, s, f], ag_send.at[2], sib_recv.at[k], sibling).start()
        else:
            to = int(way)
            remote(src, own_q.at[to, 0, 0], ag_send.at[3], own_recv.at[to, 0, 0], across[to]).start()

    def chunk(k, side):
        return (2 * k + side) * CHUNK

    def scores(k, side):
        base = chunk(k, side)
        blocks = own_q if side else sib_q
        if side:
            for b in range(4):
                arrive(k, b // 2, b % 2)
        else:
            landed(sib_q.at[k], sib_recv.at[k])
        parts = []
        for b in range(4):
            block = blocks[k, b // 2, b % 2]
            lanes_of = [block[4 * d : 4 * d + 4].reshape(ROWS, 128) for d in range(WIDTH // 128)]
            all_q[base + ROWS * b : base + ROWS * (b + 1), :] = jnp.concatenate(lanes_of, axis=1)
            meta = block[TILES].astype(jnp.float32)
            parts += [meta] + [pltpu.roll(meta, 128 - 32 * g, 1) for g in range(1, 4)]
        meta = jnp.concatenate(parts, axis=0)
        lane = lax.broadcasted_iota(jnp.int32, (1, 128), 1)
        names = jnp.where(lane < 16, meta, -1.0)
        places = (meta * 256.0 + pltpu.roll(meta, 128 - 4, 1)).astype(jnp.int32) - me * (OWNED * LABELS)
        q = all_q[base : base + CHUNK, :]
        ids = lax.broadcasted_iota(jnp.int32, (1, LABELS), 1)
        for j in range(OWNED):
            same = (names == (me * OWNED + j).astype(jnp.float32)).astype(jnp.float32)
            live = 0.5 * jnp.max(same, axis=1, keepdims=True)
            hit = None
            for w in range(4):
                one = places[:, 16 + w : 17 + w] == ids + j * LABELS
                hit = one if hit is None else jnp.logical_or(hit, one)
            s = dot(q, w_all[j * LABELS : (j + 1) * LABELS, :], 1, 1)
            g = live * jnp.tanh(s) + jnp.where(hit, live - 1.0, live)
            g_all[base : base + CHUNK, j * LABELS : (j + 1) * LABELS] = g.astype(jnp.bfloat16)

    def partial(k, side):
        base = chunk(k, side)
        return dot(g_all[base : base + CHUNK, :], w_all[...], 1, 0)

    def rs(kind, k, src, dst, device):
        remote(src, dst, rs_send.at[kind], rs_recv.at[kind, k], device).start()

    def part_sib(k):
        sib_out[k] = partial(k, 0).astype(jnp.bfloat16)
        rs(0, k, sib_out.at[k], sib_in.at[k], sibling)

    def part_own(k):
        landed(sib_in.at[k], rs_recv.at[0, k])
        plane[k] = (partial(k, 1) + sib_in[k].astype(jnp.float32)).astype(jnp.bfloat16)
        rs(1, k, plane.at[k, pl.ds(3 * ROWS, ROWS)], s_in.at[k, pl.ds(ROWS, ROWS)], second)

    def rest_second(k):
        remote(
            plane.at[k, pl.ds(2 * ROWS, ROWS)], s_in.at[k, pl.ds(0, ROWS)], rs_send.at[1], rs_recv.at[4, k], second
        ).start()

    def to_first(k):
        landed(s_in.at[k, pl.ds(ROWS, ROWS)], rs_recv.at[1, k])
        pair[k] = add_rounded(plane[k, ROWS : 2 * ROWS], s_in[k, ROWS:])
        rs(2, k, pair.at[k], f_in.at[k], first)

    def to_across(k):
        landed(s_in.at[k, pl.ds(0, ROWS)], rs_recv.at[4, k])
        landed(f_in.at[k], rs_recv.at[2, k])
        both = plane[k, :ROWS].astype(jnp.float32) + s_in[k, :ROWS].astype(jnp.float32)
        single[k] = (both + f_in[k].astype(jnp.float32)).astype(jnp.bfloat16)
        if k:
            rs(3, k, single.at[k], z_in.at[k], across[k])

    def weights_tile(j):
        rows = CHUNK
        r = dot(g_all[:, j * rows : (j + 1) * rows], all_q[...], 0, 0)
        gw_out[j * rows : (j + 1) * rows, :] = (r * 2.0).astype(jnp.bfloat16)

    actions = {
        "ss": lambda k: scores(k, 0),
        "so": lambda k: scores(k, 1),
        "ps": part_sib,
        "po": part_own,
        "pp": rest_second,
        "s2": to_first,
        "s1": to_across,
        "w": weights_tile,
    }
    waiting = [w_copy]
    for name in SCHEDULE:
        if name[0].isdigit():
            forward(int(name[0]), int(name[1]), int(name[2]), name[3])
            continue
        if waiting:
            waiting.pop().wait()
        actions[name[:-1]](int(name[-1]))
    total = single[0].astype(jnp.float32)
    for k in (1, 2, 3):
        landed(z_in.at[k], rs_recv.at[3, k])
        total = total + z_in[k].astype(jnp.float32)
    gq_out[...] = total.astype(jnp.bfloat16)
    all_sent(own_q.at[0], ag_send.at[0])
    all_sent(own_q.at[pl.ds(0, 2)], ag_send.at[1])
    all_sent(own_q, ag_send.at[2])
    all_sent(own_q.at[pl.ds(0, 3), 0, 0], ag_send.at[3])
    all_sent(sib_out, rs_send.at[0])
    all_sent(s_in, rs_send.at[1])
    all_sent(f_in, rs_send.at[2])
    all_sent(z_in.at[pl.ds(0, 3)], rs_send.at[3])


def fused_body(queries, weights, shortlist, pos_rank, pos_label):
    vmem = pl.BlockSpec(memory_space=pltpu.VMEM)
    anywhere = pl.BlockSpec(memory_space=pl.ANY)
    bf16 = jnp.bfloat16
    grad_weights, grad_queries = pl.pallas_call(
        fused_kernel,
        in_specs=[vmem] * 4 + [anywhere],
        out_specs=[vmem, vmem],
        out_shape=[
            pltpu.VMEM((OWNED * LABELS, WIDTH), bf16),
            pltpu.VMEM((ROWS, WIDTH), bf16),
        ],
        scratch_shapes=[
            pltpu.VMEM((STEPS, 2, 2, TILES + 1, 16, 128), bf16),
            pltpu.VMEM((STEPS, 2, 2, TILES + 1, 16, 128), bf16),
            pltpu.VMEM((TOTAL, WIDTH), bf16),
            pltpu.VMEM((OWNED * LABELS, WIDTH), bf16),
            pltpu.VMEM((TOTAL, OWNED * LABELS), bf16),
            pltpu.VMEM((STEPS, CHUNK, WIDTH), bf16),
            pltpu.VMEM((STEPS, CHUNK, WIDTH), bf16),
            pltpu.VMEM((STEPS, CHUNK, WIDTH), bf16),
            pltpu.VMEM((STEPS, 2 * ROWS, WIDTH), bf16),
            pltpu.VMEM((STEPS, ROWS, WIDTH), bf16),
            pltpu.VMEM((STEPS, ROWS, WIDTH), bf16),
            pltpu.VMEM((STEPS, ROWS, WIDTH), bf16),
            pltpu.VMEM((STEPS, ROWS, WIDTH), bf16),
            pltpu.SemaphoreType.DMA((4,)),
            pltpu.SemaphoreType.DMA((STEPS, 2, 2)),
            pltpu.SemaphoreType.DMA((STEPS,)),
            pltpu.SemaphoreType.DMA((4,)),
            pltpu.SemaphoreType.DMA((5, STEPS)),
            pltpu.SemaphoreType.DMA,
        ],
        cost_estimate=pl.CostEstimate(
            flops=6 * TOTAL * OWNED * LABELS * WIDTH, bytes_accessed=12 << 20, transcendentals=TOTAL * OWNED * LABELS
        ),
        compiler_params=pltpu.CompilerParams(
            collective_id=0, has_side_effects=True, vmem_limit_bytes=56 * 1024 * 1024
        ),
    )(queries, shortlist.T, pos_rank.T, pos_label.T, weights.reshape(OWNED * LABELS, WIDTH))
    return grad_weights.reshape(weights.shape), grad_queries


def body(queries, weights, shortlist, pos_rank, pos_label):
    sizes = (lax.axis_size("pb"), lax.axis_size("col")) + queries.shape + weights.shape
    sizes += (shortlist.shape[1], pos_rank.shape[1])
    if sizes == (4, 8, ROWS, WIDTH, OWNED, LABELS, WIDTH, 16, 4):
        return fused_body(queries, weights, shortlist, pos_rank, pos_label)
    return plain_body(queries, weights, shortlist, pos_rank, pos_label)


def solution(mesh):
    return jax.shard_map(
        body,
        mesh=mesh,
        in_specs=(
            P(("pb", "col"), None),
            P(("pb", "col"), None, None),
            P(("pb", "col"), None),
            P(("pb", "col"), None),
            P(("pb", "col"), None),
        ),
        out_specs=(P(("pb", "col"), None, None), P(("pb", "col"), None)),
        check_vma=False,
    )
```

```python
import functools

import jax
import jax.numpy as jnp
from jax import lax
from jax.experimental import pallas as pl
from jax.experimental.pallas import tpu as pltpu
from jax.sharding import PartitionSpec as P

META = 128
MESH = pl.DeviceIdType.MESH


def query_meta(shortlist, pos_rank, pos_label):
    top_count = shortlist.shape[1]
    rank_ids = lax.broadcasted_iota(jnp.int32, (1, 1, top_count), 2)
    chosen = jnp.sum(jnp.where(pos_rank[:, :, None] == rank_ids, shortlist[:, None, :], 0), axis=2)
    fields = [shortlist // 256, shortlist % 256, chosen // 256, chosen % 256]
    fields += [pos_label // 256, pos_label % 256]
    packed = jnp.concatenate(fields, axis=1)
    packed = jnp.pad(packed, ((0, 0), (0, META - packed.shape[1])))
    return packed.astype(jnp.float32).astype(jnp.bfloat16)


def gradient_block(meta, scores, first_cluster, owned, labels, top_count, positives):
    meta = meta.astype(jnp.float32)
    first = first_cluster.astype(jnp.float32)
    t, p = top_count, positives
    named = meta[:, :t] * 256.0 + meta[:, t : 2 * t] - first
    base = 2 * t
    at_cluster = meta[:, base : base + p] * 256.0 + meta[:, base + p : base + 2 * p] - first
    at_label = meta[:, base + 2 * p : base + 3 * p] * 256.0 + meta[:, base + 3 * p : base + 4 * p]
    places = (at_cluster * labels + at_label).astype(jnp.int32)
    label_ids = lax.broadcasted_iota(jnp.int32, (1, labels), 1)
    columns = []
    for j in range(owned):
        live = jnp.max((named == float(j)).astype(jnp.float32), axis=1, keepdims=True)
        hit = None
        for w in range(p):
            same = (places[:, w : w + 1] - j * labels) == label_ids
            hit = same if hit is None else jnp.logical_or(hit, same)
        part = scores[:, j * labels : (j + 1) * labels]
        sig = 0.5 * jnp.tanh(0.5 * part) + 0.5
        columns.append(((sig - hit.astype(jnp.float32)) * live).astype(jnp.bfloat16))
    return jnp.concatenate(columns, axis=1)


def dense_kernel(owned, labels, top_count, positives, q_ref, m_ref, w_ref, gw_ref, part_ref, acc):
    step = pl.program_id(0)
    me = lax.axis_index("pb") * lax.axis_size("col") + lax.axis_index("col")

    @pl.when(step == 0)
    def _():
        acc[...] = jnp.zeros_like(acc)

    q = q_ref[...]
    scores = lax.dot_general(q, w_ref[...], (((1,), (1,)), ((), ())), preferred_element_type=jnp.float32)
    g = gradient_block(m_ref[...], scores, me * owned, owned, labels, top_count, positives)
    part_ref[...] = jnp.dot(g, w_ref[...], preferred_element_type=jnp.float32).astype(jnp.bfloat16)
    acc[...] += lax.dot_general(g, q, (((0,), (0,)), ((), ())), preferred_element_type=jnp.float32)

    @pl.when(step == pl.num_programs(0) - 1)
    def _():
        gw_ref[...] = acc[...].astype(jnp.bfloat16)


def plain_body(queries, weights, shortlist, pos_rank, pos_label):
    rows, width = queries.shape
    owned, labels, _ = weights.shape
    pb_count, col_count = lax.axis_size("pb"), lax.axis_size("col")
    devices = pb_count * col_count
    sent = jnp.concatenate([queries, query_meta(shortlist, pos_rank, pos_label)], axis=1)
    everyone = lax.all_gather(sent, ("pb", "col"), axis=0, tiled=True)
    total = devices * rows
    block = 256
    grad_weights, part = pl.pallas_call(
        functools.partial(dense_kernel, owned, labels, shortlist.shape[1], pos_rank.shape[1]),
        grid=(total // block,),
        in_specs=[
            pl.BlockSpec((block, width), lambda i: (i, 0)),
            pl.BlockSpec((block, META), lambda i: (i, width // META)),
            pl.BlockSpec((owned * labels, width), lambda i: (0, 0)),
        ],
        out_specs=[
            pl.BlockSpec((owned * labels, width), lambda i: (0, 0)),
            pl.BlockSpec((block, width), lambda i: (i, 0)),
        ],
        out_shape=[
            jax.ShapeDtypeStruct((owned * labels, width), jnp.bfloat16),
            jax.ShapeDtypeStruct((total, width), jnp.bfloat16),
        ],
        scratch_shapes=[pltpu.VMEM((owned * labels, width), jnp.float32)],
        compiler_params=pltpu.CompilerParams(vmem_limit_bytes=60 * 1024 * 1024),
    )(everyone, everyone, weights.reshape(owned * labels, width))
    part = part.reshape(pb_count, col_count, rows, width)
    part = lax.all_to_all(part, "pb", split_axis=0, concat_axis=0, tiled=True)
    part = jnp.sum(part, axis=0, dtype=jnp.float32).astype(jnp.bfloat16)
    part = lax.all_to_all(part, "col", split_axis=0, concat_axis=0, tiled=True)
    grad_queries = jnp.sum(part, axis=0, dtype=jnp.float32).astype(jnp.bfloat16)
    return grad_weights.reshape(weights.shape), grad_queries


def dot(a, b, ca, cb):
    return lax.dot_general(a, b, (((ca,), (cb,)), ((), ())), preferred_element_type=jnp.float32)


def add_rounded(a, b):
    return (a.astype(jnp.float32) + b.astype(jnp.float32)).astype(jnp.bfloat16)


STEPS = 4
ROWS = 64
CHUNK = 256
HALF = 128
WIDTH = 1024
LABELS = 512
OWNED = 4
TOTAL = 2048
TILES = 32


SCHEDULE = (
    "0001", "000s", "000f", "0002", "t0", "001s", "100f", "001b", "100s", "0003", "011b", "so0", "200f", "ss0",
    "101s", "ps0", "101b", "201s", "201b", "200s", "111b", "so1", "300f", "ss1", "211b", "300s", "ps1", "301s", "ss2",
    "po1", "ps2", "301b", "so2", "pp1", "311b", "po2", "ss3", "pp2", "s21", "ps3", "s22", "so3", "po3", "po0", "s12",
    "pp3", "w6", "s23", "s11", "w7", "w2", "s20", "pp0", "s13", "w5", "w1", "w4", "w3", "w0", "s10",
)


def fused_kernel(
    q_ref, sl_ref, pr_ref, lab_ref, w_hbm,
    gw_out, gq_out,
    own_q, sib_q, all_q, w_all, w_t, g_all,
    sib_out, sib_in, plane, s_in, pair, f_in, single, z_in,
    ag_send, own_recv, sib_recv, pair_recv, rs_send, rs_recv, w_sem,
):
    pb, col = lax.axis_index("pb"), lax.axis_index("col")
    core = pb % 2
    x, z = col % 2, col // 2
    flip_y, flip_x = (pb + 2) % 4, col + 1 - 2 * x
    first = (pb + core * (flip_y - pb), col + (1 - core) * (flip_x - col))
    second = (pb + (1 - core) * (flip_y - pb), col + core * (flip_x - col))
    sibling = (pb + 1 - 2 * core, col)
    zs = [z, z + 1 - 2 * (z % 2), (z + 2) % 4, 3 - z]
    across = [None] + [(pb, zs[k] * 2 + x) for k in (1, 2, 3)]
    me = pb * lax.axis_size("col") + col

    barrier = pltpu.get_barrier_semaphore()
    partners = [first, second, sibling] + across[1:]
    for partner in partners:
        pl.semaphore_signal(barrier, inc=1, device_id=partner, device_id_type=MESH)

    w_copy = pltpu.make_async_copy(w_hbm, w_all, w_sem)
    w_copy.start()

    half = (q_ref[...].astype(jnp.float32) * 0.5).astype(jnp.bfloat16)
    for d in range(WIDTH // 128):
        own_q[0, 0, 0, 4 * d : 4 * d + 4] = half[:, 128 * d : 128 * (d + 1)].reshape(4, 16, 128)
    named = sl_ref[...]
    rank_ids = lax.broadcasted_iota(jnp.int32, (16, 1), 0)
    rows_of = lax.broadcasted_iota(jnp.int32, (8, 1), 0)
    places = jnp.zeros((8, ROWS), jnp.int32)
    for j in range(4):
        chosen = jnp.sum(jnp.where(pr_ref[j : j + 1, :] == rank_ids, named, 0), axis=0, keepdims=True)
        place = chosen * LABELS + lab_ref[j : j + 1, :]
        places = jnp.where(rows_of == j, place >> 8, places)
        places = jnp.where(rows_of == 4 + j, place & 255, places)
    fields = jnp.concatenate([named, places, jnp.zeros((104, ROWS), jnp.int32)], axis=0).astype(jnp.float32)
    fields = jnp.concatenate([fields, jnp.zeros((128, 128 - ROWS), jnp.float32)], axis=1).T
    tile = fields[0:16]
    for g in range(1, 4):
        tile = tile + pltpu.roll(fields[16 * g : 16 * g + 16], 32 * g, 1)
    own_q[0, 0, 0, TILES] = tile.astype(jnp.bfloat16)

    pl.semaphore_wait(barrier, len(partners))

    def remote(src, dst, send_sem, recv_sem, device):
        return pltpu.make_async_remote_copy(
            src_ref=src, dst_ref=dst, send_sem=send_sem, recv_sem=recv_sem, device_id=device, device_id_type=MESH
        )

    def landed(ref, recv_sem):
        remote(ref, ref, w_sem, recv_sem, sibling).wait_recv()

    def all_sent(ref, send_sem):
        remote(ref, ref, send_sem, w_sem, sibling).wait_send()

    arrived = []

    def arrive(k, s, f):
        if k + s + f and not any(done == (k, s, f) for done in arrived):
            arrived.append((k, s, f))
            landed(own_q.at[k, s, f], own_recv.at[k, s, f])

    def forward(k, s, f, way):
        arrive(k, s, f)
        src = own_q.at[k, s, f]
        if way == "f":
            remote(src, own_q.at[k, s, 1], ag_send.at[0], own_recv.at[k, s, 1], first).start()
        elif way == "s":
            remote(src, own_q.at[k, 1, f], ag_send.at[1], own_recv.at[k, 1, f], second).start()
        elif way == "b":
            arrive(k, s, 0)
            remote(own_q.at[k, s], sib_q.at[k, s], ag_send.at[2], sib_recv.at[k, s], sibling).start()
        else:
            to = int(way)
            remote(src, own_q.at[to, 0, 0], ag_send.at[3], own_recv.at[to, 0, 0], across[to]).start()

    def rows_of_step(k, side, halves):
        start = (2 * k + side) * CHUNK + halves[0] * HALF
        return slice(start, start + len(halves) * HALF)

    def transpose():
        for j in range(OWNED):
            w_t[:, j * LABELS : (j + 1) * LABELS] = w_all[j * LABELS : (j + 1) * LABELS, :].T

    def scores(k, side, halves):
        blocks = own_q if side else sib_q
        for h in halves:
            if side:
                arrive(k, h, 0)
                arrive(k, h, 1)
            else:
                landed(sib_q.at[k, h], sib_recv.at[k, h])
        where = rows_of_step(k, side, halves)
        parts, queries = [], []
        for h in halves:
            for f in range(2):
                block = blocks[k, h, f]
                lanes_of = [block[4 * d : 4 * d + 4].reshape(ROWS, 128) for d in range(WIDTH // 128)]
                queries.append(jnp.concatenate(lanes_of, axis=1))
                meta = block[TILES].astype(jnp.float32)
                parts += [meta] + [pltpu.roll(meta, 128 - 32 * g, 1) for g in range(1, 4)]
        all_q[where, :] = jnp.concatenate(queries, axis=0)
        meta = jnp.concatenate(parts, axis=0)
        lane = lax.broadcasted_iota(jnp.int32, (1, 128), 1)
        names = jnp.where(lane < 16, meta, -1.0)
        places = (meta * 256.0 + pltpu.roll(meta, 128 - 4, 1)).astype(jnp.int32) - me * (OWNED * LABELS)
        q = all_q[where, :]
        ids = lax.broadcasted_iota(jnp.int32, (1, LABELS), 1)
        for j in range(OWNED):
            same = (names == (me * OWNED + j).astype(jnp.float32)).astype(jnp.float32)
            live = 0.5 * jnp.max(same, axis=1, keepdims=True)
            hit = None
            for w in range(4):
                one = places[:, 16 + w : 17 + w] == ids + j * LABELS
                hit = one if hit is None else jnp.logical_or(hit, one)
            s = dot(q, w_t[:, j * LABELS : (j + 1) * LABELS], 1, 0)
            g = live * jnp.tanh(s) + jnp.where(hit, live - 1.0, live)
            g_all[where, j * LABELS : (j + 1) * LABELS] = g.astype(jnp.bfloat16)

    def partial(k, side, halves):
        return dot(g_all[rows_of_step(k, side, halves), :], w_all[...], 1, 0)

    def rs(kind, k, src, dst, device):
        remote(src, dst, rs_send.at[kind], rs_recv.at[kind, k], device).start()

    def part_sib(k, halves):
        part = partial(k, 0, halves).astype(jnp.bfloat16)
        for n, h in enumerate(halves):
            sib_out[k, h] = part[n * HALF : (n + 1) * HALF]
        if len(halves) == 2:
            remote(sib_out.at[k], sib_in.at[k], rs_send.at[0], pair_recv.at[k, 0], sibling).start()
        else:
            h = halves[0]
            remote(sib_out.at[k, h], sib_in.at[k, h], rs_send.at[0], pair_recv.at[k, h], sibling).start()

    def part_own(k, halves):
        if len(halves) == 2:
            landed(sib_in.at[k], pair_recv.at[k, 0])
        else:
            landed(sib_in.at[k, halves[0]], pair_recv.at[k, halves[0]])
        part = partial(k, 1, halves)
        for n, h in enumerate(halves):
            both = part[n * HALF : (n + 1) * HALF] + sib_in[k, h].astype(jnp.float32)
            plane[k, h * HALF : (h + 1) * HALF] = both.astype(jnp.bfloat16)
        if 1 in halves:
            rs(1, k, plane.at[k, pl.ds(3 * ROWS, ROWS)], s_in.at[k, pl.ds(ROWS, ROWS)], second)

    def rest_second(k):
        remote(
            plane.at[k, pl.ds(2 * ROWS, ROWS)], s_in.at[k, pl.ds(0, ROWS)], rs_send.at[1], rs_recv.at[4, k], second
        ).start()

    def to_first(k):
        landed(s_in.at[k, pl.ds(ROWS, ROWS)], rs_recv.at[1, k])
        pair[k] = add_rounded(plane[k, ROWS : 2 * ROWS], s_in[k, ROWS:])
        rs(2, k, pair.at[k], f_in.at[k], first)

    def to_across(k):
        landed(s_in.at[k, pl.ds(0, ROWS)], rs_recv.at[4, k])
        landed(f_in.at[k], rs_recv.at[2, k])
        both = plane[k, :ROWS].astype(jnp.float32) + s_in[k, :ROWS].astype(jnp.float32)
        single[k] = (both + f_in[k].astype(jnp.float32)).astype(jnp.bfloat16)
        if k:
            rs(3, k, single.at[k], z_in.at[k], across[k])

    def weights_tile(j):
        rows = CHUNK
        r = dot(g_all[:, j * rows : (j + 1) * rows], all_q[...], 0, 0)
        gw_out[j * rows : (j + 1) * rows, :] = (r * 2.0).astype(jnp.bfloat16)

    both = (0, 1)
    actions = {
        "ss": lambda k, halves: scores(k, 0, halves),
        "so": lambda k, halves: scores(k, 1, halves),
        "ps": part_sib,
        "po": part_own,
        "pp": lambda k, halves: rest_second(k),
        "s2": lambda k, halves: to_first(k),
        "s1": lambda k, halves: to_across(k),
    }
    for name in SCHEDULE:
        if name[0].isdigit():
            forward(int(name[0]), int(name[1]), int(name[2]), name[3])
        elif name[0] == "t":
            w_copy.wait()
            transpose()
        elif name[0] == "w":
            weights_tile(int(name[1]))
        else:
            actions[name[:2]](int(name[2]), (int(name[3]),) if name[3:] else both)
    total = single[0].astype(jnp.float32)
    for k in (1, 2, 3):
        landed(z_in.at[k], rs_recv.at[3, k])
        total = total + z_in[k].astype(jnp.float32)
    gq_out[...] = total.astype(jnp.bfloat16)
    all_sent(own_q.at[0], ag_send.at[0])
    all_sent(own_q.at[pl.ds(0, 2)], ag_send.at[1])
    all_sent(own_q, ag_send.at[2])
    all_sent(own_q.at[pl.ds(0, 3), 0, 0], ag_send.at[3])
    all_sent(sib_out, rs_send.at[0])
    all_sent(s_in, rs_send.at[1])
    all_sent(f_in, rs_send.at[2])
    all_sent(z_in.at[pl.ds(0, 3)], rs_send.at[3])


def fused_body(queries, weights, shortlist, pos_rank, pos_label):
    vmem = pl.BlockSpec(memory_space=pltpu.VMEM)
    anywhere = pl.BlockSpec(memory_space=pl.ANY)
    bf16 = jnp.bfloat16
    grad_weights, grad_queries = pl.pallas_call(
        fused_kernel,
        in_specs=[vmem] * 4 + [anywhere],
        out_specs=[vmem, vmem],
        out_shape=[
            pltpu.VMEM((OWNED * LABELS, WIDTH), bf16),
            pltpu.VMEM((ROWS, WIDTH), bf16),
        ],
        scratch_shapes=[
            pltpu.VMEM((STEPS, 2, 2, TILES + 1, 16, 128), bf16),
            pltpu.VMEM((STEPS, 2, 2, TILES + 1, 16, 128), bf16),
            pltpu.VMEM((TOTAL, WIDTH), bf16),
            pltpu.VMEM((OWNED * LABELS, WIDTH), bf16),
            pltpu.VMEM((WIDTH, OWNED * LABELS), bf16),
            pltpu.VMEM((TOTAL, OWNED * LABELS), bf16),
            pltpu.VMEM((STEPS, 2, HALF, WIDTH), bf16),
            pltpu.VMEM((STEPS, 2, HALF, WIDTH), bf16),
            pltpu.VMEM((STEPS, CHUNK, WIDTH), bf16),
            pltpu.VMEM((STEPS, 2 * ROWS, WIDTH), bf16),
            pltpu.VMEM((STEPS, ROWS, WIDTH), bf16),
            pltpu.VMEM((STEPS, ROWS, WIDTH), bf16),
            pltpu.VMEM((STEPS, ROWS, WIDTH), bf16),
            pltpu.VMEM((STEPS, ROWS, WIDTH), bf16),
            pltpu.SemaphoreType.DMA((4,)),
            pltpu.SemaphoreType.DMA((STEPS, 2, 2)),
            pltpu.SemaphoreType.DMA((STEPS, 2)),
            pltpu.SemaphoreType.DMA((STEPS, 2)),
            pltpu.SemaphoreType.DMA((4,)),
            pltpu.SemaphoreType.DMA((5, STEPS)),
            pltpu.SemaphoreType.DMA,
        ],
        cost_estimate=pl.CostEstimate(
            flops=6 * TOTAL * OWNED * LABELS * WIDTH, bytes_accessed=12 << 20, transcendentals=TOTAL * OWNED * LABELS
        ),
        compiler_params=pltpu.CompilerParams(
            collective_id=0, has_side_effects=True, vmem_limit_bytes=56 * 1024 * 1024
        ),
    )(queries, shortlist.T, pos_rank.T, pos_label.T, weights.reshape(OWNED * LABELS, WIDTH))
    return grad_weights.reshape(weights.shape), grad_queries


def body(queries, weights, shortlist, pos_rank, pos_label):
    sizes = (lax.axis_size("pb"), lax.axis_size("col")) + queries.shape + weights.shape
    sizes += (shortlist.shape[1], pos_rank.shape[1])
    if sizes == (4, 8, ROWS, WIDTH, OWNED, LABELS, WIDTH, 16, 4):
        return fused_body(queries, weights, shortlist, pos_rank, pos_label)
    return plain_body(queries, weights, shortlist, pos_rank, pos_label)


def solution(mesh):
    return jax.shard_map(
        body,
        mesh=mesh,
        in_specs=(
            P(("pb", "col"), None),
            P(("pb", "col"), None, None),
            P(("pb", "col"), None),
            P(("pb", "col"), None),
            P(("pb", "col"), None),
        ),
        out_specs=(P(("pb", "col"), None, None), P(("pb", "col"), None)),
        check_vma=False,
    )
```

```python
import functools

import jax
import jax.numpy as jnp
from jax import lax
from jax.experimental import pallas as pl
from jax.experimental.pallas import tpu as pltpu
from jax.sharding import PartitionSpec as P

META = 128
MESH = pl.DeviceIdType.MESH


def query_meta(shortlist, pos_rank, pos_label):
    top_count = shortlist.shape[1]
    rank_ids = lax.broadcasted_iota(jnp.int32, (1, 1, top_count), 2)
    chosen = jnp.sum(jnp.where(pos_rank[:, :, None] == rank_ids, shortlist[:, None, :], 0), axis=2)
    fields = [shortlist // 256, shortlist % 256, chosen // 256, chosen % 256]
    fields += [pos_label // 256, pos_label % 256]
    packed = jnp.concatenate(fields, axis=1)
    packed = jnp.pad(packed, ((0, 0), (0, META - packed.shape[1])))
    return packed.astype(jnp.float32).astype(jnp.bfloat16)


def gradient_block(meta, scores, first_cluster, owned, labels, top_count, positives):
    meta = meta.astype(jnp.float32)
    first = first_cluster.astype(jnp.float32)
    t, p = top_count, positives
    named = meta[:, :t] * 256.0 + meta[:, t : 2 * t] - first
    base = 2 * t
    at_cluster = meta[:, base : base + p] * 256.0 + meta[:, base + p : base + 2 * p] - first
    at_label = meta[:, base + 2 * p : base + 3 * p] * 256.0 + meta[:, base + 3 * p : base + 4 * p]
    places = (at_cluster * labels + at_label).astype(jnp.int32)
    label_ids = lax.broadcasted_iota(jnp.int32, (1, labels), 1)
    columns = []
    for j in range(owned):
        live = jnp.max((named == float(j)).astype(jnp.float32), axis=1, keepdims=True)
        hit = None
        for w in range(p):
            same = (places[:, w : w + 1] - j * labels) == label_ids
            hit = same if hit is None else jnp.logical_or(hit, same)
        part = scores[:, j * labels : (j + 1) * labels]
        sig = 0.5 * jnp.tanh(0.5 * part) + 0.5
        columns.append(((sig - hit.astype(jnp.float32)) * live).astype(jnp.bfloat16))
    return jnp.concatenate(columns, axis=1)


def dense_kernel(owned, labels, top_count, positives, q_ref, m_ref, w_ref, gw_ref, part_ref, acc):
    step = pl.program_id(0)
    me = lax.axis_index("pb") * lax.axis_size("col") + lax.axis_index("col")

    @pl.when(step == 0)
    def _():
        acc[...] = jnp.zeros_like(acc)

    q = q_ref[...]
    scores = lax.dot_general(q, w_ref[...], (((1,), (1,)), ((), ())), preferred_element_type=jnp.float32)
    g = gradient_block(m_ref[...], scores, me * owned, owned, labels, top_count, positives)
    part_ref[...] = jnp.dot(g, w_ref[...], preferred_element_type=jnp.float32).astype(jnp.bfloat16)
    acc[...] += lax.dot_general(g, q, (((0,), (0,)), ((), ())), preferred_element_type=jnp.float32)

    @pl.when(step == pl.num_programs(0) - 1)
    def _():
        gw_ref[...] = acc[...].astype(jnp.bfloat16)


def plain_body(queries, weights, shortlist, pos_rank, pos_label):
    rows, width = queries.shape
    owned, labels, _ = weights.shape
    pb_count, col_count = lax.axis_size("pb"), lax.axis_size("col")
    devices = pb_count * col_count
    sent = jnp.concatenate([queries, query_meta(shortlist, pos_rank, pos_label)], axis=1)
    everyone = lax.all_gather(sent, ("pb", "col"), axis=0, tiled=True)
    total = devices * rows
    block = 256
    grad_weights, part = pl.pallas_call(
        functools.partial(dense_kernel, owned, labels, shortlist.shape[1], pos_rank.shape[1]),
        grid=(total // block,),
        in_specs=[
            pl.BlockSpec((block, width), lambda i: (i, 0)),
            pl.BlockSpec((block, META), lambda i: (i, width // META)),
            pl.BlockSpec((owned * labels, width), lambda i: (0, 0)),
        ],
        out_specs=[
            pl.BlockSpec((owned * labels, width), lambda i: (0, 0)),
            pl.BlockSpec((block, width), lambda i: (i, 0)),
        ],
        out_shape=[
            jax.ShapeDtypeStruct((owned * labels, width), jnp.bfloat16),
            jax.ShapeDtypeStruct((total, width), jnp.bfloat16),
        ],
        scratch_shapes=[pltpu.VMEM((owned * labels, width), jnp.float32)],
        compiler_params=pltpu.CompilerParams(vmem_limit_bytes=60 * 1024 * 1024),
    )(everyone, everyone, weights.reshape(owned * labels, width))
    part = part.reshape(pb_count, col_count, rows, width)
    part = lax.all_to_all(part, "pb", split_axis=0, concat_axis=0, tiled=True)
    part = jnp.sum(part, axis=0, dtype=jnp.float32).astype(jnp.bfloat16)
    part = lax.all_to_all(part, "col", split_axis=0, concat_axis=0, tiled=True)
    grad_queries = jnp.sum(part, axis=0, dtype=jnp.float32).astype(jnp.bfloat16)
    return grad_weights.reshape(weights.shape), grad_queries


def dot(a, b, ca, cb):
    return lax.dot_general(a, b, (((ca,), (cb,)), ((), ())), preferred_element_type=jnp.float32)


def add_rounded(a, b):
    return (a.astype(jnp.float32) + b.astype(jnp.float32)).astype(jnp.bfloat16)


STEPS = 4
ROWS = 64
CHUNK = 256
HALF = 128
WIDTH = 1024
LABELS = 512
OWNED = 4
TOTAL = 2048
TILES = 32


SCHEDULE = (
    "0001", "000s", "000f", "0002", "001s", "100f", "t0", "001b", "100s", "0003", "011b", "so0", "200f", "ss0",
    "101s", "ps0", "101b", "201s", "201b", "200s", "111b", "so1", "300f", "ss1", "211b", "300s", "ps1", "301s", "ss2",
    "po1", "ps2", "301b", "so2", "pp1", "311b", "po2", "ss3", "pp2", "s21", "ps3", "s22", "so3", "po3", "po0", "s12",
    "pp3", "w6", "s23", "s11", "w7", "w2", "s20", "pp0", "s13", "w5", "w1", "w4", "w3", "w0", "s10",
)


def fused_kernel(
    q_ref, sl_ref, pr_ref, lab_ref, w_hbm,
    gw_out, gq_out,
    own_q, sib_q, all_q, w_all, w_t, g_all,
    sib_out, sib_in, plane, s_in, pair, f_in, single, z_in,
    ag_send, own_recv, sib_recv, pair_recv, rs_send, rs_recv, w_sem,
):
    pb, col = lax.axis_index("pb"), lax.axis_index("col")
    core = pb % 2
    x, z = col % 2, col // 2
    flip_y, flip_x = (pb + 2) % 4, col + 1 - 2 * x
    first = (pb + core * (flip_y - pb), col + (1 - core) * (flip_x - col))
    second = (pb + (1 - core) * (flip_y - pb), col + core * (flip_x - col))
    sibling = (pb + 1 - 2 * core, col)
    zs = [z, z + 1 - 2 * (z % 2), (z + 2) % 4, 3 - z]
    across = [None] + [(pb, zs[k] * 2 + x) for k in (1, 2, 3)]
    me = pb * lax.axis_size("col") + col

    barrier = pltpu.get_barrier_semaphore()
    partners = [first, second, sibling] + across[1:]
    for partner in partners:
        pl.semaphore_signal(barrier, inc=1, device_id=partner, device_id_type=MESH)

    w_copy = pltpu.make_async_copy(w_hbm, w_all, w_sem)
    w_copy.start()

    half = (q_ref[...].astype(jnp.float32) * 0.5).astype(jnp.bfloat16)
    for d in range(WIDTH // 128):
        own_q[0, 0, 0, 4 * d : 4 * d + 4] = half[:, 128 * d : 128 * (d + 1)].reshape(4, 16, 128)
    named = sl_ref[...]
    rank_ids = lax.broadcasted_iota(jnp.int32, (16, 1), 0)
    rows_of = lax.broadcasted_iota(jnp.int32, (8, 1), 0)
    places = jnp.zeros((8, ROWS), jnp.int32)
    for j in range(4):
        chosen = jnp.sum(jnp.where(pr_ref[j : j + 1, :] == rank_ids, named, 0), axis=0, keepdims=True)
        place = chosen * LABELS + lab_ref[j : j + 1, :]
        places = jnp.where(rows_of == j, place >> 8, places)
        places = jnp.where(rows_of == 4 + j, place & 255, places)
    fields = jnp.concatenate([named, places, jnp.zeros((104, ROWS), jnp.int32)], axis=0).astype(jnp.float32)
    fields = jnp.concatenate([fields, jnp.zeros((128, 128 - ROWS), jnp.float32)], axis=1).T
    tile = fields[0:16]
    for g in range(1, 4):
        tile = tile + pltpu.roll(fields[16 * g : 16 * g + 16], 32 * g, 1)
    own_q[0, 0, 0, TILES] = tile.astype(jnp.bfloat16)

    pl.semaphore_wait(barrier, len(partners))

    def remote(src, dst, send_sem, recv_sem, device):
        return pltpu.make_async_remote_copy(
            src_ref=src, dst_ref=dst, send_sem=send_sem, recv_sem=recv_sem, device_id=device, device_id_type=MESH
        )

    def landed(ref, recv_sem):
        remote(ref, ref, w_sem, recv_sem, sibling).wait_recv()

    def all_sent(ref, send_sem):
        remote(ref, ref, send_sem, w_sem, sibling).wait_send()

    arrived = []

    def arrive(k, s, f):
        if k + s + f and not any(done == (k, s, f) for done in arrived):
            arrived.append((k, s, f))
            landed(own_q.at[k, s, f], own_recv.at[k, s, f])

    def forward(k, s, f, way):
        arrive(k, s, f)
        src = own_q.at[k, s, f]
        if way == "f":
            remote(src, own_q.at[k, s, 1], ag_send.at[0], own_recv.at[k, s, 1], first).start()
        elif way == "s":
            remote(src, own_q.at[k, 1, f], ag_send.at[1], own_recv.at[k, 1, f], second).start()
        elif way == "b":
            arrive(k, s, 0)
            remote(own_q.at[k, s], sib_q.at[k, s], ag_send.at[2], sib_recv.at[k, s], sibling).start()
        else:
            to = int(way)
            remote(src, own_q.at[to, 0, 0], ag_send.at[3], own_recv.at[to, 0, 0], across[to]).start()

    def rows_of_step(k, side, halves):
        start = (2 * k + side) * CHUNK + halves[0] * HALF
        return slice(start, start + len(halves) * HALF)

    def transpose():
        for j in range(OWNED):
            w_t[:, j * LABELS : (j + 1) * LABELS] = w_all[j * LABELS : (j + 1) * LABELS, :].T

    def scores(k, side, halves):
        blocks = own_q if side else sib_q
        for h in halves:
            if side:
                arrive(k, h, 0)
                arrive(k, h, 1)
            else:
                landed(sib_q.at[k, h], sib_recv.at[k, h])
        where = rows_of_step(k, side, halves)
        parts, queries = [], []
        for h in halves:
            for f in range(2):
                block = blocks[k, h, f]
                lanes_of = [block[4 * d : 4 * d + 4].reshape(ROWS, 128) for d in range(WIDTH // 128)]
                queries.append(jnp.concatenate(lanes_of, axis=1))
                meta = block[TILES].astype(jnp.float32)
                parts += [meta] + [pltpu.roll(meta, 128 - 32 * g, 1) for g in range(1, 4)]
        all_q[where, :] = jnp.concatenate(queries, axis=0)
        meta = jnp.concatenate(parts, axis=0)
        lane = lax.broadcasted_iota(jnp.int32, (1, 128), 1)
        names = jnp.where(lane < 16, meta, -1.0)
        places = (meta * 256.0 + pltpu.roll(meta, 128 - 4, 1)).astype(jnp.int32) - me * (OWNED * LABELS)
        q = all_q[where, :]
        ids = lax.broadcasted_iota(jnp.int32, (1, LABELS), 1)
        for j in range(OWNED):
            same = (names == (me * OWNED + j).astype(jnp.float32)).astype(jnp.float32)
            live = 0.5 * jnp.max(same, axis=1, keepdims=True)
            hit = None
            for w in range(4):
                one = places[:, 16 + w : 17 + w] == ids + j * LABELS
                hit = one if hit is None else jnp.logical_or(hit, one)
            s = dot(q, w_t[:, j * LABELS : (j + 1) * LABELS], 1, 0)
            g = live * jnp.tanh(s) + jnp.where(hit, live - 1.0, live)
            g_all[where, j * LABELS : (j + 1) * LABELS] = g.astype(jnp.bfloat16)

    def partial(k, side, halves):
        return dot(g_all[rows_of_step(k, side, halves), :], w_all[...], 1, 0)

    def rs(kind, k, src, dst, device):
        remote(src, dst, rs_send.at[kind], rs_recv.at[kind, k], device).start()

    def part_sib(k, halves):
        part = partial(k, 0, halves).astype(jnp.bfloat16)
        for n, h in enumerate(halves):
            sib_out[k, h] = part[n * HALF : (n + 1) * HALF]
        if len(halves) == 2:
            remote(sib_out.at[k], sib_in.at[k], rs_send.at[0], pair_recv.at[k, 0], sibling).start()
        else:
            h = halves[0]
            remote(sib_out.at[k, h], sib_in.at[k, h], rs_send.at[0], pair_recv.at[k, h], sibling).start()

    def part_own(k, halves):
        if len(halves) == 2:
            landed(sib_in.at[k], pair_recv.at[k, 0])
        else:
            landed(sib_in.at[k, halves[0]], pair_recv.at[k, halves[0]])
        part = partial(k, 1, halves)
        for n, h in enumerate(halves):
            both = part[n * HALF : (n + 1) * HALF] + sib_in[k, h].astype(jnp.float32)
            plane[k, h * HALF : (h + 1) * HALF] = both.astype(jnp.bfloat16)
        if 1 in halves:
            rs(1, k, plane.at[k, pl.ds(3 * ROWS, ROWS)], s_in.at[k, pl.ds(ROWS, ROWS)], second)

    def rest_second(k):
        remote(
            plane.at[k, pl.ds(2 * ROWS, ROWS)], s_in.at[k, pl.ds(0, ROWS)], rs_send.at[1], rs_recv.at[4, k], second
        ).start()

    def to_first(k):
        landed(s_in.at[k, pl.ds(ROWS, ROWS)], rs_recv.at[1, k])
        pair[k] = add_rounded(plane[k, ROWS : 2 * ROWS], s_in[k, ROWS:])
        rs(2, k, pair.at[k], f_in.at[k], first)

    def to_across(k):
        landed(s_in.at[k, pl.ds(0, ROWS)], rs_recv.at[4, k])
        landed(f_in.at[k], rs_recv.at[2, k])
        both = plane[k, :ROWS].astype(jnp.float32) + s_in[k, :ROWS].astype(jnp.float32)
        single[k] = (both + f_in[k].astype(jnp.float32)).astype(jnp.bfloat16)
        if k:
            rs(3, k, single.at[k], z_in.at[k], across[k])

    def weights_tile(j):
        rows = CHUNK
        r = dot(g_all[:, j * rows : (j + 1) * rows], all_q[...], 0, 0)
        gw_out[j * rows : (j + 1) * rows, :] = (r * 2.0).astype(jnp.bfloat16)

    both = (0, 1)
    actions = {
        "ss": lambda k, halves: scores(k, 0, halves),
        "so": lambda k, halves: scores(k, 1, halves),
        "ps": part_sib,
        "po": part_own,
        "pp": lambda k, halves: rest_second(k),
        "s2": lambda k, halves: to_first(k),
        "s1": lambda k, halves: to_across(k),
    }
    for name in SCHEDULE:
        if name[0].isdigit():
            forward(int(name[0]), int(name[1]), int(name[2]), name[3])
        elif name[0] == "t":
            w_copy.wait()
            transpose()
        elif name[0] == "w":
            weights_tile(int(name[1]))
        else:
            actions[name[:2]](int(name[2]), (int(name[3]),) if name[3:] else both)
    total = single[0].astype(jnp.float32)
    for k in (1, 2, 3):
        landed(z_in.at[k], rs_recv.at[3, k])
        total = total + z_in[k].astype(jnp.float32)
    gq_out[...] = total.astype(jnp.bfloat16)
    all_sent(own_q.at[0], ag_send.at[0])
    all_sent(own_q.at[pl.ds(0, 2)], ag_send.at[1])
    all_sent(own_q, ag_send.at[2])
    all_sent(own_q.at[pl.ds(0, 3), 0, 0], ag_send.at[3])
    all_sent(sib_out, rs_send.at[0])
    all_sent(s_in, rs_send.at[1])
    all_sent(f_in, rs_send.at[2])
    all_sent(z_in.at[pl.ds(0, 3)], rs_send.at[3])


def fused_body(queries, weights, shortlist, pos_rank, pos_label):
    vmem = pl.BlockSpec(memory_space=pltpu.VMEM)
    anywhere = pl.BlockSpec(memory_space=pl.ANY)
    bf16 = jnp.bfloat16
    grad_weights, grad_queries = pl.pallas_call(
        fused_kernel,
        in_specs=[vmem] * 4 + [anywhere],
        out_specs=[vmem, vmem],
        out_shape=[
            pltpu.VMEM((OWNED * LABELS, WIDTH), bf16),
            pltpu.VMEM((ROWS, WIDTH), bf16),
        ],
        scratch_shapes=[
            pltpu.VMEM((STEPS, 2, 2, TILES + 1, 16, 128), bf16),
            pltpu.VMEM((STEPS, 2, 2, TILES + 1, 16, 128), bf16),
            pltpu.VMEM((TOTAL, WIDTH), bf16),
            pltpu.VMEM((OWNED * LABELS, WIDTH), bf16),
            pltpu.VMEM((WIDTH, OWNED * LABELS), bf16),
            pltpu.VMEM((TOTAL, OWNED * LABELS), bf16),
            pltpu.VMEM((STEPS, 2, HALF, WIDTH), bf16),
            pltpu.VMEM((STEPS, 2, HALF, WIDTH), bf16),
            pltpu.VMEM((STEPS, CHUNK, WIDTH), bf16),
            pltpu.VMEM((STEPS, 2 * ROWS, WIDTH), bf16),
            pltpu.VMEM((STEPS, ROWS, WIDTH), bf16),
            pltpu.VMEM((STEPS, ROWS, WIDTH), bf16),
            pltpu.VMEM((STEPS, ROWS, WIDTH), bf16),
            pltpu.VMEM((STEPS, ROWS, WIDTH), bf16),
            pltpu.SemaphoreType.DMA((4,)),
            pltpu.SemaphoreType.DMA((STEPS, 2, 2)),
            pltpu.SemaphoreType.DMA((STEPS, 2)),
            pltpu.SemaphoreType.DMA((STEPS, 2)),
            pltpu.SemaphoreType.DMA((4,)),
            pltpu.SemaphoreType.DMA((5, STEPS)),
            pltpu.SemaphoreType.DMA,
        ],
        cost_estimate=pl.CostEstimate(
            flops=6 * TOTAL * OWNED * LABELS * WIDTH, bytes_accessed=12 << 20, transcendentals=TOTAL * OWNED * LABELS
        ),
        compiler_params=pltpu.CompilerParams(
            collective_id=0, has_side_effects=True, vmem_limit_bytes=59 * 1024 * 1024
        ),
    )(queries, shortlist.T, pos_rank.T, pos_label.T, weights.reshape(OWNED * LABELS, WIDTH))
    return grad_weights.reshape(weights.shape), grad_queries


def body(queries, weights, shortlist, pos_rank, pos_label):
    sizes = (lax.axis_size("pb"), lax.axis_size("col")) + queries.shape + weights.shape
    sizes += (shortlist.shape[1], pos_rank.shape[1])
    if sizes == (4, 8, ROWS, WIDTH, OWNED, LABELS, WIDTH, 16, 4):
        return fused_body(queries, weights, shortlist, pos_rank, pos_label)
    return plain_body(queries, weights, shortlist, pos_rank, pos_label)


def solution(mesh):
    return jax.shard_map(
        body,
        mesh=mesh,
        in_specs=(
            P(("pb", "col"), None),
            P(("pb", "col"), None, None),
            P(("pb", "col"), None),
            P(("pb", "col"), None),
            P(("pb", "col"), None),
        ),
        out_specs=(P(("pb", "col"), None, None), P(("pb", "col"), None)),
        check_vma=False,
    )
```
